32 devices in a mesh: band: 2 (over y), mesh: 16 (over z, x, core).
Axes of the slice: x: 2, y: 2, z: 4, core: 2. Of those that a mesh axis runs over, the one named last changes fastest.
Arguments:
- psi: bfloat16 [16, 1536, 1536], P('mesh', 'band'), may hold values from -6 to 6
- ritz: bfloat16 [1536, 1536], replicated, may hold values from -0.15625 to 0.15625
- cell_ham: bfloat16 [16, 4, 512, 512], P('mesh'), may hold values from -0.25 to 0.25
- cell_nodes: int32 [16, 4, 512], P('mesh'), may hold values from 0 to 1535, as said below
- face_nodes: int32 [16, 4, 256], P('mesh'), may hold values from 0 to 1535, as said below
Outputs:
- filtered: bfloat16 [16, 1536, 1536], P('mesh', None, 'band')
The draws below stay inside these ranges and needn't reach their ends.
Inputs may be any that keep to these rules, and one draw needn't show every extreme that they name: `cell_nodes`: each row of 512 entries names distinct local nodes, and every local node lies in some cell of its partition. `face_nodes`: the 1024 entries of one partition name distinct local nodes.
All inputs are finite; a program needn't handle non-finite values.
Results may differ from the reference program's by a relative error of at most 0.0058.
Values may be sent and summed in bfloat16 or wider, within the bound.
A program may use at most 64 MiB of HBM per device.

```python
import jax
import jax.numpy as jnp
from jax import lax

BANDS = 1536
NODES_CELL = 512
CELLS = 4
GRID_W = 4
NLOC = 1536
SHARED = 256
PARTS_SIZE = 16


def draw_cell_nodes(key, part):
    part_keys = jax.random.split(key, PARTS_SIZE)
    orderings = jax.vmap(lambda sub: jax.random.permutation(sub, NLOC))(part_keys)
    starts = jnp.arange(CELLS) * (NLOC - NODES_CELL) // (CELLS - 1)
    positions = starts[:, None] + jnp.arange(NODES_CELL)[None, :]
    return orderings[:, positions].astype(jnp.int32)


def draw_face_nodes(key, part):
    base_key = jax.random.fold_in(key, 7)
    part_keys = jax.random.split(base_key, PARTS_SIZE)

    def one_part(sub):
        ordering = jax.random.permutation(sub, NLOC)
        pick_at = jax.random.randint(jax.random.fold_in(sub, 3), (), 0, 4 * SHARED)
        positions = jnp.arange(NLOC)
        swapped = jnp.where(positions == pick_at, NLOC - 1, jnp.where(ordering == NLOC - 1, ordering[pick_at], ordering))
        return swapped[:4 * SHARED].reshape(4, SHARED)
    return jax.vmap(one_part)(part_keys).astype(jnp.int32)


def steps_of(rng, shape, cuts, low, top_value):
    factor_of = 1.0
    for dim, shards_of in cuts:
        heights = jax.random.uniform(jax.random.fold_in(jax.random.fold_in(rng, 6), dim), (shards_of,), jnp.float32, low / len(cuts), top_value / len(cuts))
        factor_of = factor_of * jnp.repeat(jnp.exp(heights), shape[dim] // shards_of).reshape((-1,) + (1,) * (len(shape) - 1 - dim))
    return factor_of


def centred(rng, dims, deviation, most, cuts=(), kind=jnp.bfloat16):
    result = deviation * jax.random.normal(rng, dims, jnp.float32)
    if cuts:
        result = result * steps_of(rng, dims, cuts, -0.22, 0.18)
    return jnp.clip(result, -most, most).astype(kind)


def setup_inputs(seed: int = 0) -> dict:
    key_list = jax.random.split(jax.random.key(seed), 6)
    return {
        "psi": centred(key_list[0], (PARTS_SIZE, NLOC, BANDS), 1.0, 6.0, ((0, 16), (1, 2))),
        "ritz": centred(key_list[1], (BANDS, BANDS), BANDS ** -0.5, 0.15625),
        "cell_ham": centred(key_list[2], (PARTS_SIZE, CELLS, NODES_CELL, NODES_CELL), NODES_CELL ** -0.5, 0.25, ((0, 16),)),
        "cell_nodes": draw_cell_nodes(jax.random.fold_in(key_list[5], 71), 0),
        "face_nodes": draw_face_nodes(jax.random.fold_in(key_list[5], 71), 0),
    }


def cell_products(vectors, cell_ham, cell_nodes):
    def one_part(items):
        part_vec, part_ham, part_nodes = items
        picked = part_vec[part_nodes].astype(jnp.float32)
        products = jnp.einsum("cij,cjb->cib", part_ham.astype(jnp.float32), picked)
        summed = jnp.zeros((NLOC, BANDS), jnp.float32)
        return summed.at[part_nodes.reshape(-1)].add(products.reshape(-1, BANDS))
    return lax.map(one_part, (vectors, cell_ham, cell_nodes))


def assemble(summed, face_nodes):
    rounded = lax.optimization_barrier(summed.astype(jnp.bfloat16)).astype(jnp.float32)
    flat_faces = face_nodes.reshape(PARTS_SIZE, 4 * SHARED)
    blocks = jax.vmap(lambda part_vals, rows: part_vals[rows])(rounded, flat_faces)
    blocks = blocks.reshape(PARTS_SIZE, 4, SHARED, BANDS)
    from_left = jnp.roll(blocks[:, 1], 1, axis=0)
    from_right = jnp.roll(blocks[:, 0], -1, axis=0)
    from_below = jnp.roll(blocks[:, 3], GRID_W, axis=0)
    from_above = jnp.roll(blocks[:, 2], -GRID_W, axis=0)
    arrived = jnp.stack([from_left, from_right, from_below, from_above], axis=1).reshape(PARTS_SIZE, 4 * SHARED, BANDS)
    return jax.vmap(lambda part_sum, rows, extra: part_sum.at[rows].add(extra))(summed, flat_faces, arrived)


def operator(vectors, cell_ham, cell_nodes, face_nodes):
    return assemble(cell_products(vectors, cell_ham, cell_nodes), face_nodes)


def reference(psi, ritz, cell_ham, cell_nodes, face_nodes):
    rotated = jnp.dot(psi.reshape(PARTS_SIZE * NLOC, BANDS), ritz, preferred_element_type=jnp.float32)
    rotated = rotated.astype(jnp.bfloat16).reshape(PARTS_SIZE, NLOC, BANDS)
    applied = operator(rotated, cell_ham, cell_nodes, face_nodes)
    first = ((applied - 0.25 * rotated.astype(jnp.float32)) / 2.0).astype(jnp.bfloat16)
    applied_next = operator(first, cell_ham, cell_nodes, face_nodes)
    filtered = 2.0 * (applied_next - 0.25 * first.astype(jnp.float32)) / 2.0 - rotated.astype(jnp.float32)
    return filtered.astype(jnp.bfloat16)
```

```python
import functools
import math

import jax
import jax.numpy as jnp
from jax import lax
from jax.experimental import pallas as pl
from jax.experimental.pallas import tpu as pltpu
from jax.sharding import PartitionSpec as P

GRID_W = 4
MESH = pl.DeviceIdType.MESH
BF16 = jnp.bfloat16
F32 = jnp.float32


def dot(a, b):
    return jnp.dot(a, b, preferred_element_type=F32)


def hot(condition):
    return jnp.where(condition, 1.0, 0.0).astype(BF16)


def upright(row):
    return jnp.broadcast_to(row, (128, row.shape[1])).T


def across(column, width):
    return jnp.concatenate([column] * (width // 128), axis=1)


def chunks_of(group):
    wide = 256 if group % 256 == 0 else 128
    return [(at, wide) for at in range(0, group, wide)]


def kernel(bands, parts, psi_hbm, ritz_hbm, ham_hbm, cell_nodes, face_nodes, out,
           psi, ritz, ham, turned, arrived, rotated, first, summed, leaving, landing,
           cell_hot, picked, dense, order_hot, place_hot, columns,
           load, store, row_send, row_recv, face_send, face_recv):
    me_b = lax.axis_index("band")
    me_p = lax.axis_index("mesh")
    rows = psi.shape[0]
    nloc = rows * bands
    group = ritz.shape[2]
    chunks = chunks_of(group)
    count = len(chunks)
    shared = face_nodes.shape[1]
    face_rows = 4 * shared
    cells, size = ham.shape[0], ham.shape[1]
    total = cells * size
    tile = math.gcd(2 * shared, nloc)
    step = 256

    routes = ((3, 2, GRID_W), (2, 3, -GRID_W), (1, 0, 1), (0, 1, -1))

    def part(offset):
        return lax.rem(me_p + offset + parts, parts)

    def partner(offset):
        return lax.rem(me_b + offset, bands)

    def ritz_load(offset):
        at = pl.multiple_of(partner(offset) * group, 128)
        return pltpu.make_async_copy(ritz_hbm.at[:, pl.ds(at, group)], ritz.at[offset], load.at[2 + offset])

    psi_load = pltpu.make_async_copy(psi_hbm, psi, load.at[0])
    ham_load = pltpu.make_async_copy(ham_hbm, ham, load.at[1])
    psi_load.start()
    for offset in range(1, bands):
        ritz_load(offset).start()
    ham_load.start()
    ritz_load(0).start()

    barrier = pltpu.get_barrier_semaphore()
    for offset in range(1, bands):
        pl.semaphore_signal(barrier, inc=1, device_id=(partner(offset), me_p), device_id_type=MESH)
    for _, _, offset in routes:
        pl.semaphore_signal(barrier, inc=1, device_id=(me_b, part(offset)), device_id_type=MESH)

    def own_rows(k, owner):
        return arrived[k].at[pl.ds(pl.multiple_of(owner * rows, rows), rows), :]

    def row_copy(k, offset):
        return pltpu.make_async_remote_copy(
            src_ref=turned[k].at[offset - 1],
            dst_ref=own_rows(k, me_b),
            send_sem=row_send.at[offset - 1, k],
            recv_sem=row_recv.at[offset - 1, k],
            device_id=(partner(offset), me_p),
            device_id_type=MESH,
        )

    def cut(k):
        return slice(chunks[k][0], chunks[k][0] + chunks[k][1])

    def turn(k):
        if k < count:
            for offset in range(1, bands):
                turned[k][offset - 1] = dot(psi[...], ritz[offset, :, cut(k)]).astype(BF16)
                row_copy(k, offset).start()

    def keep(k):
        if k < count:
            own_rows(k, me_b)[...] = dot(psi[...], ritz[0, :, cut(k)]).astype(BF16)

    def face_copy(turn, k, route):
        block, slot, offset = route
        return pltpu.make_async_remote_copy(
            src_ref=leaving[k].at[turn, block],
            dst_ref=landing[k].at[turn, slot],
            send_sem=face_send.at[turn, k, slot],
            recv_sem=face_recv.at[turn, k, slot],
            device_id=(me_b, part(offset)),
            device_id_type=MESH,
        )

    def operate_faces(turn, k, vectors, half):
        for at in range(half * 2 * shared, (half + 1) * 2 * shared, tile):
            part_sum = dot(dense[at:at + tile, :], vectors[...])
            summed[k][at:at + tile, :] = part_sum
            rounded = part_sum.astype(BF16)
            for block in range(4):
                low = max(at, block * shared)
                high = min(at + tile, (block + 1) * shared)
                if low < high:
                    leaving[k][turn, block, low - block * shared:high - block * shared, :] = rounded[low - at:high - at]
        for early in (True, False):
            for route in routes:
                if route[0] // 2 == half:
                    target = me_p + route[2]
                    wraps = jnp.logical_or(target < 0, target >= parts)

                    @pl.when(wraps if early else jnp.logical_not(wraps))
                    def _(route=route):
                        face_copy(turn, k, route).start()

    def receive(k):
        for offset in range(1, bands):
            row_copy(k, offset).wait()

    def pick(at, node):
        for cell in range(cells):
            span = slice(cell * size, (cell + 1) * size)
            picked[:, span] = dot(hot(node(at) == cell_nodes[cell:cell + 1, :]), ham[cell]).astype(BF16)

    def fill(at):
        for to in range(0, nloc, step):
            dense[at:at + tile, to:to + step] = dot(picked[...], cell_hot[:, to:to + step]).astype(BF16)

    def face_node(at):
        return across(columns[at:at + tile, :], size)

    for face in range(4):
        columns[face * shared:(face + 1) * shared, :] = upright(face_nodes[face:face + 1, :])
    for cell in range(cells):
        at = face_rows + cell * size
        columns[at:at + size, :] = upright(cell_nodes[cell:cell + 1, :])

    psi_load.wait()
    for offset in range(1, bands):
        ritz_load(offset).wait()
    pl.semaphore_wait(barrier, bands + 3)
    turn(0)
    ham_load.wait()
    pick(2 * shared, face_node)
    turn(1)

    @pl.loop(0, total // step)
    def _(r):
        at = pl.multiple_of(r * step, step)
        numbers = lax.broadcasted_iota(jnp.int32, (step, nloc), 1)
        cell_hot[pl.ds(at, step), :] = hot(numbers == across(columns[pl.ds(face_rows + at, step), :], nloc))

    fill(2 * shared)
    ritz_load(0).wait()
    keep(0)
    pick(0, face_node)
    fill(0)
    receive(0)
    operate_faces(0, 0, arrived[0], 0)
    operate_faces(0, 0, arrived[0], 1)
    for k in range(2, count):
        turn(k)

    def find_face(block, found):
        at = pl.multiple_of(block * step, step)
        numbers = lax.broadcasted_iota(jnp.int32, (step, nloc), 1)
        match = jnp.where(across(columns[pl.ds(at, step), :], nloc) == numbers, 1.0, 0.0)
        order_hot[pl.ds(at, step), :] = match.astype(BF16)
        return found + jnp.sum(match, axis=0, keepdims=True)

    found = lax.fori_loop(0, face_rows // step, find_face, jnp.zeros((1, nloc), F32))
    inner = jnp.where(found == 0.0, 1, 0)
    before = jnp.broadcast_to(inner, (8, nloc))
    eight = lax.broadcasted_iota(jnp.int32, (8, nloc), 1)
    shift = 1
    while shift < nloc:
        before = before + jnp.where(eight >= shift, pltpu.roll(before, shift, 1), 0)
        shift *= 2
    place = jnp.where(found == 0.0, before[:1, :] + (face_rows - 1), -1)

    for at in range(face_rows, nloc, step):
        across_nodes = lax.broadcasted_iota(jnp.int32, (step, nloc), 1)
        match = lax.broadcasted_iota(jnp.int32, (step, nloc), 0) + at == place
        order_hot[at:at + step, :] = hot(match)
        node = jnp.sum(jnp.where(match, across_nodes, 0), axis=1, keepdims=True)
        columns[at:at + step, :] = jnp.broadcast_to(node, (step, 128))

    for at in range(face_rows, nloc, tile):
        pick(at, face_node)
        fill(at)

    columns[:nloc, :] = upright(place)
    for face in range(4):
        span = slice(face * shared, (face + 1) * shared)
        numbers = lax.broadcasted_iota(jnp.int32, (nloc, shared), 0)
        place_hot[:, span] = hot(numbers == face_nodes[face:face + 1, :])
    numbers = lax.broadcasted_iota(jnp.int32, (nloc, nloc - face_rows), 1) + face_rows
    place_hot[:, face_rows:] = hot(numbers == across(columns[:nloc, :], nloc - face_rows))

    def order(k):
        for at in range(0, nloc, tile):
            rotated[k][at:at + tile, :] = dot(order_hot[at:at + tile, :], arrived[k][...]).astype(BF16)

    def inner_first(k):
        for at in range(face_rows, nloc, tile):
            part_sum = dot(dense[at:at + tile, :], arrived[k][...])
            first[k][at:at + tile, :] = ((part_sum - 0.25 * rotated[k][at:at + tile, :].astype(F32)) / 2.0).astype(BF16)

    def assembled(turn, k, slot):
        at = slice(slot * shared, (slot + 1) * shared)
        return summed[k][at, :] + landing[k][turn, slot].astype(F32)

    def result(value, k, at):
        return (2.0 * (value - 0.25 * first[k][at, :].astype(F32)) / 2.0 - rotated[k][at, :].astype(F32)).astype(BF16)

    def advance(k):
        for route in routes[::-1]:
            face_copy(0, k, route).wait()
            at = slice(route[1] * shared, (route[1] + 1) * shared)
            first[k][at, :] = ((assembled(0, k, route[1]) - 0.25 * rotated[k][at, :].astype(F32)) / 2.0).astype(BF16)
        for at in range(0, nloc, tile):
            arrived[k][at:at + tile, :] = dot(place_hot[at:at + tile, :], first[k][...]).astype(BF16)
        operate_faces(1, k, arrived[k], 0)
        operate_faces(1, k, arrived[k], 1)

    def put(k):
        return pltpu.make_async_copy(arrived[k], out.at[:, cut(k)], store.at[k])

    def inner_result(k):
        for at in range(face_rows, nloc, tile):
            part_sum = dot(dense[at:at + tile, :], arrived[k][...])
            rotated[k][at:at + tile, :] = result(part_sum, k, slice(at, at + tile))

    def finish(k):
        for route in routes[::-1]:
            face_copy(1, k, route).wait()
            at = slice(route[1] * shared, (route[1] + 1) * shared)
            rotated[k][at, :] = result(assembled(1, k, route[1]), k, at)
        for at in range(0, nloc, tile):
            arrived[k][at:at + tile, :] = dot(place_hot[at:at + tile, :], rotated[k][...]).astype(BF16)
        put(k).start()

    keep(1)
    order(0)
    inner_first(0)
    for k in range(1, count):
        receive(k)
        operate_faces(0, k, arrived[k], 0)
        operate_faces(0, k, arrived[k], 1)
        keep(k + 1)
        advance(k - 1)
        order(k)
        inner_first(k)
    for k in range(count - 1):
        inner_result(k)
    advance(count - 1)
    for k in range(count - 1):
        finish(k)
    inner_result(count - 1)
    finish(count - 1)
    for k in range(count):
        put(k).wait()


def copy_kernel(source, target, held, taken, given):
    pieces, rows = held.shape[0], held.shape[1]

    def take(i):
        return pltpu.make_async_copy(source.at[i * rows:(i + 1) * rows, :], held.at[i], taken.at[i])

    def give(i):
        return pltpu.make_async_copy(held.at[i], target.at[i * rows:(i + 1) * rows, :], given.at[i])

    for i in range(pieces):
        take(i).start()
    for i in range(pieces):
        take(i).wait()
        give(i).start()
    for i in range(pieces):
        give(i).wait()


def local(bands, parts, psi, ritz, cell_ham, cell_nodes, face_nodes):
    rows = psi.shape[1]
    nloc = rows * bands
    group = ritz.shape[1] // bands
    cells, size = cell_ham.shape[1], cell_ham.shape[2]
    shared = face_nodes.shape[2]
    chunks = chunks_of(group)
    count = len(chunks)
    tile = math.gcd(2 * shared, nloc)
    anywhere = pl.BlockSpec(memory_space=pl.ANY)
    vmem = pl.BlockSpec(memory_space=pltpu.VMEM)

    def each(*shape, kind=BF16):
        return [pltpu.VMEM((*shape, width), kind) for _, width in chunks]

    out = pl.pallas_call(
        functools.partial(kernel, bands, parts),
        out_shape=jax.ShapeDtypeStruct((nloc, group), BF16),
        in_specs=[anywhere] * 3 + [vmem] * 2,
        out_specs=anywhere,
        scratch_shapes=[
            pltpu.VMEM((rows, ritz.shape[0]), BF16),
            pltpu.VMEM((bands, ritz.shape[0], group), BF16),
            pltpu.VMEM((cells, size, size), BF16),
            each(bands - 1, rows),
            each(nloc),
            each(nloc),
            each(nloc),
            each(4 * shared, kind=F32),
            each(2, 4, shared),
            each(2, 4, shared),
            pltpu.VMEM((cells * size, nloc), BF16),
            pltpu.VMEM((tile, cells * size), BF16),
            pltpu.VMEM((nloc, nloc), BF16),
            pltpu.VMEM((nloc, nloc), BF16),
            pltpu.VMEM((nloc, nloc), BF16),
            pltpu.VMEM((4 * shared + cells * size, 128), jnp.int32),
            pltpu.SemaphoreType.DMA((2 + bands,)),
            pltpu.SemaphoreType.DMA((count,)),
            pltpu.SemaphoreType.DMA((bands - 1, count)),
            pltpu.SemaphoreType.DMA((bands - 1, count)),
            pltpu.SemaphoreType.DMA((2, count, 4)),
            pltpu.SemaphoreType.DMA((2, count, 4)),
        ],
        compiler_params=pltpu.CompilerParams(
            collective_id=0, has_side_effects=True, vmem_limit_bytes=62 * 1024 * 1024
        ),
    )(psi[0], ritz, cell_ham[0], cell_nodes[0], face_nodes[0])
    pieces = 6 if nloc % 48 == 0 else 1
    out = pl.pallas_call(
        copy_kernel,
        out_shape=jax.ShapeDtypeStruct((nloc, group), BF16),
        in_specs=[anywhere],
        out_specs=anywhere,
        scratch_shapes=[
            pltpu.VMEM((pieces, nloc // pieces, group), BF16),
            pltpu.SemaphoreType.DMA((pieces,)),
            pltpu.SemaphoreType.DMA((pieces,)),
        ],
    )(out)
    return out[None]


def solution(mesh):
    return jax.shard_map(
        functools.partial(local, mesh.shape["band"], mesh.shape["mesh"]),
        mesh=mesh,
        in_specs=(
            P("mesh", "band", None),
            P(),
            P("mesh", None, None, None),
            P("mesh", None, None),
            P("mesh", None, None),
        ),
        out_specs=P("mesh", None, "band"),
        check_vma=False,
    )
```

```python
import functools
import math

import jax
import jax.numpy as jnp
from jax import lax
from jax.experimental import pallas as pl
from jax.experimental.pallas import tpu as pltpu
from jax.sharding import PartitionSpec as P

GRID_W = 4
MESH = pl.DeviceIdType.MESH
BF16 = jnp.bfloat16
F32 = jnp.float32


def dot(a, b):
    return jnp.dot(a, b, preferred_element_type=F32)


def hot(condition):
    return jnp.where(condition, 1.0, 0.0).astype(BF16)


def upright(row):
    return jnp.broadcast_to(row, (128, row.shape[1])).T


def across(column, width):
    return jnp.concatenate([column] * (width // 128), axis=1)


def kernel(bands, parts, psi_hbm, ritz_hbm, ham_hbm, cell_nodes, face_nodes, out,
           psi, ritz, ham, turned, arrived, rotated, first, summed, leaving, landing,
           cell_hot, picked, dense, order_hot, place_hot, columns,
           load, store, row_send, row_recv, face_send, face_recv):
    me_b = lax.axis_index("band")
    me_p = lax.axis_index("mesh")
    rows = psi.shape[0]
    count, nloc, width = arrived.shape
    group = count * width
    shared = face_nodes.shape[1]
    face_rows = 4 * shared
    cells, size = ham.shape[0], ham.shape[1]
    total = cells * size
    tile = math.gcd(2 * shared, nloc)
    step = 256

    routes = ((3, 2, GRID_W), (2, 3, -GRID_W), (1, 0, 1), (0, 1, -1))

    def part(offset):
        return lax.rem(me_p + offset + parts, parts)

    def partner(offset):
        return lax.rem(me_b + offset, bands)

    def ritz_load(offset, k):
        start = pl.multiple_of(partner(offset) * group + k * width, 128)
        return pltpu.make_async_copy(
            ritz_hbm.at[:, pl.ds(start, width)], ritz.at[offset, k], load.at[2 + offset * count + k])

    psi_load = pltpu.make_async_copy(psi_hbm, psi, load.at[0])
    ham_load = pltpu.make_async_copy(ham_hbm, ham, load.at[1])
    psi_load.start()
    for offset in range(1, bands):
        ritz_load(offset, 0).start()
    ham_load.start()

    barrier = pltpu.get_barrier_semaphore()
    for offset in range(1, bands):
        pl.semaphore_signal(barrier, inc=1, device_id=(partner(offset), me_p), device_id_type=MESH)
    for _, _, offset in routes:
        pl.semaphore_signal(barrier, inc=1, device_id=(me_b, part(offset)), device_id_type=MESH)

    def own_rows(k, owner):
        return arrived.at[k, pl.ds(pl.multiple_of(owner * rows, rows), rows), :]

    def row_copy(k, offset):
        return pltpu.make_async_remote_copy(
            src_ref=turned.at[offset - 1, k],
            dst_ref=own_rows(k, me_b),
            send_sem=row_send.at[offset - 1, k],
            recv_sem=row_recv.at[offset - 1, k],
            device_id=(partner(offset), me_p),
            device_id_type=MESH,
        )

    def chunk(k):
        return pl.ds(pl.multiple_of(k * width, 128), width)

    def turn(k):
        for offset in range(1, bands):
            ritz_load(offset, k).wait()
            turned[offset - 1, k] = dot(psi[...], ritz[offset, k]).astype(BF16)
            row_copy(k, offset).start()

    def keep(k):
        ritz_load(0, k).wait()
        own_rows(k, me_b)[...] = dot(psi[...], ritz[0, k]).astype(BF16)

    def face_copy(turn, k, route):
        block, slot, offset = route
        return pltpu.make_async_remote_copy(
            src_ref=leaving.at[turn, k, block],
            dst_ref=landing.at[turn, k, slot],
            send_sem=face_send.at[turn, k, slot],
            recv_sem=face_recv.at[turn, k, slot],
            device_id=(me_b, part(offset)),
            device_id_type=MESH,
        )

    def operate_faces(turn, k, vectors, half):
        for at in range(half * 2 * shared, (half + 1) * 2 * shared, tile):
            part_sum = dot(dense[at:at + tile, :], vectors[k])
            summed[k, at:at + tile, :] = part_sum
            rounded = part_sum.astype(BF16)
            for block in range(4):
                low = max(at, block * shared)
                high = min(at + tile, (block + 1) * shared)
                if low < high:
                    leaving[turn, k, block, low - block * shared:high - block * shared, :] = rounded[low - at:high - at]
        for route in routes:
            if route[0] // 2 == half:
                face_copy(turn, k, route).start()

    def receive(k):
        for offset in range(1, bands):
            row_copy(k, offset).wait()

    def pick(low, high, cell):
        span = pl.ds(pl.multiple_of(cell * size, 128), size)
        node = across(columns[low:high, :], size)
        picked[:high - low, span] = dot(hot(node == cell_nodes[pl.ds(cell, 1), :]), ham[cell]).astype(BF16)

    def fill(low, high, span):
        dense[low:high, span] = dot(picked[:high - low, :], cell_hot[:, span]).astype(BF16)

    for face in range(4):
        columns[face * shared:(face + 1) * shared, :] = upright(face_nodes[face:face + 1, :])
    for cell in range(cells):
        at = nloc + cell * size
        columns[at:at + size, :] = upright(cell_nodes[cell:cell + 1, :])

    psi_load.wait()
    pl.semaphore_wait(barrier, bands + 3)
    turn(0)
    for k in range(1, count):
        for offset in range(1, bands):
            ritz_load(offset, k).start()
    for k in range(count):
        ritz_load(0, k).start()
    ham_load.wait()
    found_rows = face_rows // cells

    def pick_faces(cell, found):
        pick(0, face_rows, cell)
        at = pl.multiple_of(cell * found_rows, found_rows)
        places = lax.broadcasted_iota(jnp.int32, (found_rows, nloc), 0) + (at + 1)
        match = across(columns[pl.ds(at, found_rows), :], nloc) == lax.broadcasted_iota(jnp.int32, (found_rows, nloc), 1)
        order_hot[pl.ds(at, found_rows), :] = hot(match)
        return found + jnp.sum(jnp.where(match, places, 0), axis=0, keepdims=True)

    found = lax.fori_loop(0, cells, pick_faces, jnp.zeros((1, nloc), jnp.int32))
    if count > 1:
        turn(1)

    @pl.loop(0, nloc // step)
    def _(block):
        at = pl.multiple_of(block * step, step)
        numbers = lax.broadcasted_iota(jnp.int32, (total, step), 1) + at
        cell_hot[:, pl.ds(at, step)] = hot(numbers == across(columns[nloc:, :], step))
        fill(0, face_rows, pl.ds(at, step))

    keep(0)
    receive(0)
    operate_faces(0, 0, arrived, 0)
    operate_faces(0, 0, arrived, 1)

    @pl.loop(2, count)
    def _(k):
        turn(k)

    inner = jnp.where(found == 0, 1, 0)
    before = jnp.broadcast_to(inner, (8, nloc))
    eight = lax.broadcasted_iota(jnp.int32, (8, nloc), 1)
    shift = 1
    while shift < nloc:
        before = before + jnp.where(eight >= shift, pltpu.roll(before, shift, 1), 0)
        shift *= 2
    place = jnp.where(found == 0, before[:1, :] + (face_rows - 1), found - 1)

    @pl.loop(face_rows // step, nloc // step)
    def _(block):
        at = pl.multiple_of(block * step, step)
        nodes = lax.broadcasted_iota(jnp.int32, (step, nloc), 1)
        match = lax.broadcasted_iota(jnp.int32, (step, nloc), 0) + at == place
        order_hot[pl.ds(at, step), :] = hot(match)
        node = jnp.sum(jnp.where(match, nodes, 0), axis=1, keepdims=True)
        columns[pl.ds(at, step), :] = jnp.broadcast_to(node, (step, 128))

    @pl.loop(1, count)
    def _(k):
        keep(k)

    for low in range(face_rows, nloc, face_rows):
        high = min(low + face_rows, nloc)

        @pl.loop(0, cells)
        def _(cell, low=low, high=high):
            pick(low, high, cell)

        if high == nloc:
            columns[:nloc, :] = upright(place)

        @pl.loop(0, nloc // step)
        def _(block, low=low, high=high):
            at = pl.multiple_of(block * step, step)
            if high == nloc:
                numbers = lax.broadcasted_iota(jnp.int32, (nloc, step), 1) + at
                place_hot[:, pl.ds(at, step)] = hot(numbers == across(columns[:nloc, :], step))
            fill(low, high, pl.ds(at, step))

    def order(k):
        for at in range(0, nloc, tile):
            rotated[k, at:at + tile, :] = dot(order_hot[at:at + tile, :], arrived[k]).astype(BF16)

    def inner_first(k):
        for at in range(face_rows, nloc, tile):
            part_sum = dot(dense[at:at + tile, :], arrived[k])
            first[k, at:at + tile, :] = ((part_sum - 0.25 * rotated[k, at:at + tile, :].astype(F32)) / 2.0).astype(BF16)

    def assembled(turn, k, slot):
        at = slice(slot * shared, (slot + 1) * shared)
        return summed[k, at, :] + landing[turn, k, slot].astype(F32)

    def result(value, k, at):
        return (2.0 * (value - 0.25 * first[k, at, :].astype(F32)) / 2.0 - rotated[k, at, :].astype(F32)).astype(BF16)

    def advance(k):
        for route in routes[::-1]:
            face_copy(0, k, route).wait()
            at = slice(route[1] * shared, (route[1] + 1) * shared)
            first[k, at, :] = ((assembled(0, k, route[1]) - 0.25 * rotated[k, at, :].astype(F32)) / 2.0).astype(BF16)
        for at in range(0, nloc, tile):
            arrived[k, at:at + tile, :] = dot(place_hot[at:at + tile, :], first[k]).astype(BF16)
        operate_faces(1, k, arrived, 0)
        operate_faces(1, k, arrived, 1)

    def put(k):
        return pltpu.make_async_copy(arrived.at[k], out.at[:, chunk(k)], store.at[k])

    def inner_result(k):
        for at in range(face_rows, nloc, tile):
            part_sum = dot(dense[at:at + tile, :], arrived[k])
            rotated[k, at:at + tile, :] = result(part_sum, k, slice(at, at + tile))

    def finish(k):
        for route in routes[::-1]:
            face_copy(1, k, route).wait()
            at = slice(route[1] * shared, (route[1] + 1) * shared)
            rotated[k, at, :] = result(assembled(1, k, route[1]), k, at)
        for at in range(0, nloc, tile):
            arrived[k, at:at + tile, :] = dot(place_hot[at:at + tile, :], rotated[k]).astype(BF16)
        put(k).start()

    @pl.loop(1, count + 1)
    def _(k):
        @pl.when(k < count)
        def _():
            receive(k)
            operate_faces(0, k, arrived, 0)
            operate_faces(0, k, arrived, 1)

        order(k - 1)
        inner_first(k - 1)
        advance(k - 1)
        inner_result(k - 1)

    @pl.loop(0, count)
    def _(k):
        finish(k)

    @pl.loop(0, count)
    def _(k):
        put(k).wait()


def copy_kernel(source, target, held, taken, given):
    pieces, rows = held.shape[0], held.shape[1]

    def take(i):
        return pltpu.make_async_copy(source.at[i * rows:(i + 1) * rows, :], held.at[i], taken.at[i])

    def give(i):
        return pltpu.make_async_copy(held.at[i], target.at[i * rows:(i + 1) * rows, :], given.at[i])

    for i in range(pieces):
        take(i).start()
    for i in range(pieces):
        take(i).wait()
        give(i).start()
    for i in range(pieces):
        give(i).wait()


def local(bands, parts, psi, ritz, cell_ham, cell_nodes, face_nodes):
    rows = psi.shape[1]
    nloc = rows * bands
    group = ritz.shape[1] // bands
    cells, size = cell_ham.shape[1], cell_ham.shape[2]
    shared = face_nodes.shape[2]
    width = 256 if group % 256 == 0 else 128
    count = group // width
    anywhere = pl.BlockSpec(memory_space=pl.ANY)
    vmem = pl.BlockSpec(memory_space=pltpu.VMEM)

    out = pl.pallas_call(
        functools.partial(kernel, bands, parts),
        out_shape=jax.ShapeDtypeStruct((nloc, group), BF16),
        in_specs=[anywhere] * 3 + [vmem] * 2,
        out_specs=anywhere,
        scratch_shapes=[
            pltpu.VMEM((rows, ritz.shape[0]), BF16),
            pltpu.VMEM((bands, count, ritz.shape[0], width), BF16),
            pltpu.VMEM((cells, size, size), BF16),
            pltpu.VMEM((bands - 1, count, rows, width), BF16),
            pltpu.VMEM((count, nloc, width), BF16),
            pltpu.VMEM((count, nloc, width), BF16),
            pltpu.VMEM((count, nloc, width), BF16),
            pltpu.VMEM((count, 4 * shared, width), F32),
            pltpu.VMEM((2, count, 4, shared, width), BF16),
            pltpu.VMEM((2, count, 4, shared, width), BF16),
            pltpu.VMEM((cells * size, nloc), BF16),
            pltpu.VMEM((4 * shared, cells * size), BF16),
            pltpu.VMEM((nloc, nloc), BF16),
            pltpu.VMEM((nloc, nloc), BF16),
            pltpu.VMEM((nloc, nloc), BF16),
            pltpu.VMEM((nloc + cells * size, 128), jnp.int32),
            pltpu.SemaphoreType.DMA((2 + bands * count,)),
            pltpu.SemaphoreType.DMA((count,)),
            pltpu.SemaphoreType.DMA((bands - 1, count)),
            pltpu.SemaphoreType.DMA((bands - 1, count)),
            pltpu.SemaphoreType.DMA((2, count, 4)),
            pltpu.SemaphoreType.DMA((2, count, 4)),
        ],
        compiler_params=pltpu.CompilerParams(
            collective_id=0, has_side_effects=True, vmem_limit_bytes=62 * 1024 * 1024
        ),
    )(psi[0], ritz, cell_ham[0], cell_nodes[0], face_nodes[0])
    pieces = 6 if nloc % 48 == 0 else 1
    out = pl.pallas_call(
        copy_kernel,
        out_shape=jax.ShapeDtypeStruct((nloc, group), BF16),
        in_specs=[anywhere],
        out_specs=anywhere,
        scratch_shapes=[
            pltpu.VMEM((pieces, nloc // pieces, group), BF16),
            pltpu.SemaphoreType.DMA((pieces,)),
            pltpu.SemaphoreType.DMA((pieces,)),
        ],
    )(out)
    return out[None]


def solution(mesh):
    return jax.shard_map(
        functools.partial(local, mesh.shape["band"], mesh.shape["mesh"]),
        mesh=mesh,
        in_specs=(
            P("mesh", "band", None),
            P(),
            P("mesh", None, None, None),
            P("mesh", None, None),
            P("mesh", None, None),
        ),
        out_specs=P("mesh", None, "band"),
        check_vma=False,
    )
```

```python
import functools
import math

import jax
import jax.numpy as jnp
from jax import lax
from jax.experimental import pallas as pl
from jax.experimental.pallas import tpu as pltpu
from jax.sharding import PartitionSpec as P

GRID_W = 4
MESH = pl.DeviceIdType.MESH
BF16 = jnp.bfloat16
F32 = jnp.float32


def dot(a, b):
    return jnp.dot(a, b, preferred_element_type=F32)


def hot(condition):
    return jnp.where(condition, 1.0, 0.0).astype(BF16)


def upright(row):
    return jnp.broadcast_to(row, (128, row.shape[1])).T


def across(column, width):
    return jnp.concatenate([column] * (width // 128), axis=1)


def kernel(bands, parts, psi_hbm, ritz_hbm, ham_hbm, cell_nodes, face_nodes, out,
           psi, ritz, ham, turned, arrived, rotated, first, summed, leaving, landing,
           cell_hot, picked, dense, order_hot, place_hot, columns, found,
           load, store, row_send, row_recv, face_send, face_recv):
    me_b = lax.axis_index("band")
    me_p = lax.axis_index("mesh")
    rows = psi.shape[0]
    count, nloc, width = arrived.shape
    group = count * width
    shared = face_nodes.shape[1]
    face_rows = 4 * shared
    cells, size = ham.shape[0], ham.shape[1]
    total = cells * size
    tile = math.gcd(2 * shared, nloc)
    step = 256

    routes = ((3, 2, GRID_W), (2, 3, -GRID_W), (1, 0, 1), (0, 1, -1))

    def part(offset):
        return lax.rem(me_p + offset + parts, parts)

    def partner(offset):
        return lax.rem(me_b + offset, bands)

    def ritz_load(offset, k):
        start = pl.multiple_of(partner(offset) * group + k * width, 128)
        return pltpu.make_async_copy(
            ritz_hbm.at[:, pl.ds(start, width)], ritz.at[offset, k], load.at[2 + offset * count + k])

    psi_load = pltpu.make_async_copy(psi_hbm, psi, load.at[0])
    ham_load = pltpu.make_async_copy(ham_hbm, ham, load.at[1])
    psi_load.start()
    for offset in range(1, bands):
        ritz_load(offset, 0).start()
    ham_load.start()

    barrier = pltpu.get_barrier_semaphore()
    for offset in range(1, bands):
        pl.semaphore_signal(barrier, inc=1, device_id=(partner(offset), me_p), device_id_type=MESH)
    for _, _, offset in routes:
        pl.semaphore_signal(barrier, inc=1, device_id=(me_b, part(offset)), device_id_type=MESH)

    def own_rows(k, owner):
        return arrived.at[k, pl.ds(pl.multiple_of(owner * rows, rows), rows), :]

    def row_copy(k, offset):
        return pltpu.make_async_remote_copy(
            src_ref=turned.at[offset - 1, k],
            dst_ref=own_rows(k, me_b),
            send_sem=row_send.at[offset - 1, k],
            recv_sem=row_recv.at[offset - 1, k],
            device_id=(partner(offset), me_p),
            device_id_type=MESH,
        )

    def chunk(k):
        return pl.ds(pl.multiple_of(k * width, 128), width)

    def turn(k):
        for offset in range(1, bands):
            ritz_load(offset, k).wait()
            turned[offset - 1, k] = dot(psi[...], ritz[offset, k]).astype(BF16)
            row_copy(k, offset).start()

    def keep(k):
        ritz_load(0, k).wait()
        own_rows(k, me_b)[...] = dot(psi[...], ritz[0, k]).astype(BF16)

    def face_copy(turn, k, route):
        block, slot, offset = route
        return pltpu.make_async_remote_copy(
            src_ref=leaving.at[turn, k, block],
            dst_ref=landing.at[turn, k, slot],
            send_sem=face_send.at[turn, k, slot],
            recv_sem=face_recv.at[turn, k, slot],
            device_id=(me_b, part(offset)),
            device_id_type=MESH,
        )

    def operate_faces(turn, k, vectors, half):
        for at in range(half * 2 * shared, (half + 1) * 2 * shared, tile):
            part_sum = dot(dense[at:at + tile, :], vectors[k])
            summed[k, at:at + tile, :] = part_sum
            rounded = part_sum.astype(BF16)
            for block in range(4):
                low = max(at, block * shared)
                high = min(at + tile, (block + 1) * shared)
                if low < high:
                    leaving[turn, k, block, low - block * shared:high - block * shared, :] = rounded[low - at:high - at]
        for route in routes:
            if route[0] // 2 == half:
                face_copy(turn, k, route).start()

    def receive(k):
        for offset in range(1, bands):
            row_copy(k, offset).wait()

    def pick(low, high, cell):
        span = pl.ds(pl.multiple_of(cell * size, 128), size)
        node = across(columns[low:high, :], size)
        picked[:high - low, span] = dot(hot(node == cell_nodes[pl.ds(cell, 1), :]), ham[cell]).astype(BF16)

    def fill(low, high, span):
        dense[low:high, span] = dot(picked[:high - low, :], cell_hot[:, span]).astype(BF16)

    for face in range(4):
        columns[face * shared:(face + 1) * shared, :] = upright(face_nodes[face:face + 1, :])
    for cell in range(cells):
        at = nloc + cell * size
        columns[at:at + size, :] = upright(cell_nodes[cell:cell + 1, :])

    psi_load.wait()
    pl.semaphore_wait(barrier, bands + 3)
    turn(0)
    for k in range(1, count):
        for offset in range(1, bands):
            ritz_load(offset, k).start()
    for k in range(count):
        ritz_load(0, k).start()
    ham_load.wait()
    half = 2 * shared

    @pl.loop(0, cells, unroll=2)
    def _(cell):
        pick(half, face_rows, cell)

    if count > 1:
        turn(1)

    @pl.loop(0, nloc // step, unroll=2)
    def _(block):
        at = pl.multiple_of(block * step, step)
        numbers = lax.broadcasted_iota(jnp.int32, (total, step), 1) + at
        cell_hot[:, pl.ds(at, step)] = hot(numbers == across(columns[nloc:, :], step))
        fill(half, face_rows, pl.ds(at, step))

    keep(0)

    @pl.loop(0, cells, unroll=2)
    def _(cell):
        pick(0, half, cell)

    receive(0)
    operate_faces(0, 0, arrived, 1)

    @pl.loop(0, nloc // step, unroll=2)
    def _(block):
        at = pl.multiple_of(block * step, step)
        fill(0, half, pl.ds(at, step))
        match = lax.broadcasted_iota(jnp.int32, (face_rows, step), 1) + at == across(columns[:face_rows, :], step)
        order_hot[:face_rows, pl.ds(at, step)] = hot(match)
        places = lax.broadcasted_iota(jnp.int32, (face_rows, step), 0) + 1
        found[:, pl.ds(at, step)] = jnp.sum(jnp.where(match, places, 0), axis=0, keepdims=True)

    operate_faces(0, 0, arrived, 0)

    @pl.loop(2, count)
    def _(k):
        turn(k)

    if count > 1:
        keep(1)

    inner = jnp.where(found[...] == 0, 1, 0)
    before = jnp.broadcast_to(inner, (8, nloc))
    eight = lax.broadcasted_iota(jnp.int32, (8, nloc), 1)
    shift = 1
    while shift < nloc:
        before = before + jnp.where(eight >= shift, pltpu.roll(before, shift, 1), 0)
        shift *= 2
    place = jnp.where(found[...] == 0, before[:1, :] + (face_rows - 1), found[...] - 1)

    @pl.loop(face_rows // step, nloc // step)
    def _(block):
        at = pl.multiple_of(block * step, step)
        nodes = lax.broadcasted_iota(jnp.int32, (step, nloc), 1)
        match = lax.broadcasted_iota(jnp.int32, (step, nloc), 0) + at == place
        order_hot[pl.ds(at, step), :] = hot(match)
        node = jnp.sum(jnp.where(match, nodes, 0), axis=1, keepdims=True)
        columns[pl.ds(at, step), :] = jnp.broadcast_to(node, (step, 128))

    low = face_rows
    while low < nloc:
        high = min(low + half, nloc)

        @pl.loop(0, cells, unroll=2)
        def _(cell, low=low, high=high):
            pick(low, high, cell)

        if high == nloc:
            columns[:nloc, :] = upright(place)
        if low == face_rows and count > 1:
            receive(1)
            operate_faces(0, 1, arrived, 0)
            operate_faces(0, 1, arrived, 1)

        @pl.loop(0, nloc // step, unroll=2)
        def _(block, low=low, high=high):
            at = pl.multiple_of(block * step, step)
            if high == nloc:
                numbers = lax.broadcasted_iota(jnp.int32, (nloc, step), 1) + at
                place_hot[:, pl.ds(at, step)] = hot(numbers == across(columns[:nloc, :], step))
            fill(low, high, pl.ds(at, step))

        low = high

    def order(k):
        for at in range(0, nloc, tile):
            rotated[k, at:at + tile, :] = dot(order_hot[at:at + tile, :], arrived[k]).astype(BF16)

    def inner_first(k):
        for at in range(face_rows, nloc, tile):
            part_sum = dot(dense[at:at + tile, :], arrived[k])
            first[k, at:at + tile, :] = ((part_sum - 0.25 * rotated[k, at:at + tile, :].astype(F32)) / 2.0).astype(BF16)

    def assembled(turn, k, slot):
        at = slice(slot * shared, (slot + 1) * shared)
        return summed[k, at, :] + landing[turn, k, slot].astype(F32)

    def result(value, k, at):
        return (2.0 * (value - 0.25 * first[k, at, :].astype(F32)) / 2.0 - rotated[k, at, :].astype(F32)).astype(BF16)

    def advance(k):
        for route in routes[::-1]:
            face_copy(0, k, route).wait()
            at = slice(route[1] * shared, (route[1] + 1) * shared)
            first[k, at, :] = ((assembled(0, k, route[1]) - 0.25 * rotated[k, at, :].astype(F32)) / 2.0).astype(BF16)
        for at in range(0, nloc, tile):
            arrived[k, at:at + tile, :] = dot(place_hot[at:at + tile, :], first[k]).astype(BF16)
        operate_faces(1, k, arrived, 0)
        operate_faces(1, k, arrived, 1)

    def put(k):
        return pltpu.make_async_copy(arrived.at[k], out.at[:, chunk(k)], store.at[k])

    def inner_result(k):
        for at in range(face_rows, nloc, tile):
            part_sum = dot(dense[at:at + tile, :], arrived[k])
            rotated[k, at:at + tile, :] = result(part_sum, k, slice(at, at + tile))

    def finish(k):
        for route in routes[::-1]:
            face_copy(1, k, route).wait()
            at = slice(route[1] * shared, (route[1] + 1) * shared)
            rotated[k, at, :] = result(assembled(1, k, route[1]), k, at)
        for at in range(0, nloc, tile):
            arrived[k, at:at + tile, :] = dot(place_hot[at:at + tile, :], rotated[k]).astype(BF16)
        put(k).start()

    @pl.loop(0, count)
    def _(k):
        @pl.when(k + 2 < count)
        def _():
            keep(k + 2)
            receive(k + 2)
            operate_faces(0, k + 2, arrived, 1)
            operate_faces(0, k + 2, arrived, 0)

        order(k)
        inner_first(k)
        advance(k)
        inner_result(k)

    @pl.loop(0, count)
    def _(k):
        finish(k)

    @pl.loop(0, count)
    def _(k):
        put(k).wait()


def copy_kernel(source, target, held, taken, given):
    pieces, rows = held.shape[0], held.shape[1]

    def take(i):
        return pltpu.make_async_copy(source.at[i * rows:(i + 1) * rows, :], held.at[i], taken.at[i])

    def give(i):
        return pltpu.make_async_copy(held.at[i], target.at[i * rows:(i + 1) * rows, :], given.at[i])

    for i in range(pieces):
        take(i).start()
    for i in range(pieces):
        take(i).wait()
        give(i).start()
    for i in range(pieces):
        give(i).wait()


def local(bands, parts, psi, ritz, cell_ham, cell_nodes, face_nodes):
    rows = psi.shape[1]
    nloc = rows * bands
    group = ritz.shape[1] // bands
    cells, size = cell_ham.shape[1], cell_ham.shape[2]
    shared = face_nodes.shape[2]
    width = 256 if group % 256 == 0 else 128
    count = group // width
    anywhere = pl.BlockSpec(memory_space=pl.ANY)
    vmem = pl.BlockSpec(memory_space=pltpu.VMEM)

    out = pl.pallas_call(
        functools.partial(kernel, bands, parts),
        out_shape=jax.ShapeDtypeStruct((nloc, group), BF16),
        in_specs=[anywhere] * 3 + [vmem] * 2,
        out_specs=anywhere,
        scratch_shapes=[
            pltpu.VMEM((rows, ritz.shape[0]), BF16),
            pltpu.VMEM((bands, count, ritz.shape[0], width), BF16),
            pltpu.VMEM((cells, size, size), BF16),
            pltpu.VMEM((bands - 1, count, rows, width), BF16),
            pltpu.VMEM((count, nloc, width), BF16),
            pltpu.VMEM((count, nloc, width), BF16),
            pltpu.VMEM((count, nloc, width), BF16),
            pltpu.VMEM((count, 4 * shared, width), F32),
            pltpu.VMEM((2, count, 4, shared, width), BF16),
            pltpu.VMEM((2, count, 4, shared, width), BF16),
            pltpu.VMEM((cells * size, nloc), BF16),
            pltpu.VMEM((2 * shared, cells * size), BF16),
            pltpu.VMEM((nloc, nloc), BF16),
            pltpu.VMEM((nloc, nloc), BF16),
            pltpu.VMEM((nloc, nloc), BF16),
            pltpu.VMEM((nloc + cells * size, 128), jnp.int32),
            pltpu.VMEM((1, nloc), jnp.int32),
            pltpu.SemaphoreType.DMA((2 + bands * count,)),
            pltpu.SemaphoreType.DMA((count,)),
            pltpu.SemaphoreType.DMA((bands - 1, count)),
            pltpu.SemaphoreType.DMA((bands - 1, count)),
            pltpu.SemaphoreType.DMA((2, count, 4)),
            pltpu.SemaphoreType.DMA((2, count, 4)),
        ],
        compiler_params=pltpu.CompilerParams(
            collective_id=0, has_side_effects=True, vmem_limit_bytes=62 * 1024 * 1024
        ),
    )(psi[0], ritz, cell_ham[0], cell_nodes[0], face_nodes[0])
    pieces = 6 if nloc % 48 == 0 else 1
    out = pl.pallas_call(
        copy_kernel,
        out_shape=jax.ShapeDtypeStruct((nloc, group), BF16),
        in_specs=[anywhere],
        out_specs=anywhere,
        scratch_shapes=[
            pltpu.VMEM((pieces, nloc // pieces, group), BF16),
            pltpu.SemaphoreType.DMA((pieces,)),
            pltpu.SemaphoreType.DMA((pieces,)),
        ],
    )(out)
    return out[None]


def solution(mesh):
    return jax.shard_map(
        functools.partial(local, mesh.shape["band"], mesh.shape["mesh"]),
        mesh=mesh,
        in_specs=(
            P("mesh", "band", None),
            P(),
            P("mesh", None, None, None),
            P("mesh", None, None),
            P("mesh", None, None),
        ),
        out_specs=P("mesh", None, "band"),
        check_vma=False,
    )
```

```python
import functools
import math

import jax
import jax.numpy as jnp
from jax import lax
from jax.experimental import pallas as pl
from jax.experimental.pallas import tpu as pltpu
from jax.sharding import PartitionSpec as P

GRID_W = 4
MESH = pl.DeviceIdType.MESH
BF16 = jnp.bfloat16
F32 = jnp.float32


def dot(a, b):
    return jnp.dot(a, b, preferred_element_type=F32)


def hot(condition):
    return jnp.where(condition, 1.0, 0.0).astype(BF16)


def upright(row):
    return jnp.broadcast_to(row, (128, row.shape[1])).T


def across(column, width):
    return jnp.concatenate([column] * (width // 128), axis=1)


def kernel(bands, parts, psi_hbm, ritz_hbm, ham_hbm, cell_nodes, face_nodes, out,
           psi, ritz, ham, turned, arrived, rotated, first, summed, leaving, landing,
           cell_hot, picked, dense, order_hot, place_hot, columns, found,
           load, store, row_send, row_recv, face_send, face_recv):
    me_b = lax.axis_index("band")
    me_p = lax.axis_index("mesh")
    rows = psi.shape[0]
    count, nloc, width = arrived.shape
    group = count * width
    shared = face_nodes.shape[1]
    face_rows = 4 * shared
    cells, size = ham.shape[0], ham.shape[1]
    total = cells * size
    tile = math.gcd(2 * shared, nloc)
    step = 256

    routes = ((3, 2, GRID_W), (2, 3, -GRID_W), (1, 0, 1), (0, 1, -1))

    def part(offset):
        return lax.rem(me_p + offset + parts, parts)

    def partner(offset):
        return lax.rem(me_b + offset, bands)

    def ritz_load(offset, k):
        start = pl.multiple_of(partner(offset) * group + k * width, 128)
        return pltpu.make_async_copy(
            ritz_hbm.at[:, pl.ds(start, width)], ritz.at[offset, k], load.at[2 + offset * count + k])

    psi_load = pltpu.make_async_copy(psi_hbm, psi, load.at[0])
    ham_load = pltpu.make_async_copy(ham_hbm, ham, load.at[1])
    psi_load.start()
    for offset in range(1, bands):
        ritz_load(offset, 0).start()
    ham_load.start()

    barrier = pltpu.get_barrier_semaphore()
    for offset in range(1, bands):
        pl.semaphore_signal(barrier, inc=1, device_id=(partner(offset), me_p), device_id_type=MESH)
    for _, _, offset in routes:
        pl.semaphore_signal(barrier, inc=1, device_id=(me_b, part(offset)), device_id_type=MESH)

    def own_rows(k, owner):
        return arrived.at[k, pl.ds(pl.multiple_of(owner * rows, rows), rows), :]

    def row_copy(k, offset):
        return pltpu.make_async_remote_copy(
            src_ref=turned.at[offset - 1, k],
            dst_ref=own_rows(k, me_b),
            send_sem=row_send.at[offset - 1, k],
            recv_sem=row_recv.at[offset - 1, k],
            device_id=(partner(offset), me_p),
            device_id_type=MESH,
        )

    def chunk(k):
        return pl.ds(pl.multiple_of(k * width, 128), width)

    def turn(k):
        for offset in range(1, bands):
            ritz_load(offset, k).wait()
            turned[offset - 1, k] = dot(psi[...], ritz[offset, k]).astype(BF16)
            row_copy(k, offset).start()

    def keep(k):
        ritz_load(0, k).wait()
        own_rows(k, me_b)[...] = dot(psi[...], ritz[0, k]).astype(BF16)

    def face_copy(turn, k, route):
        block, slot, offset = route
        return pltpu.make_async_remote_copy(
            src_ref=leaving.at[turn, k, block],
            dst_ref=landing.at[turn, k, slot],
            send_sem=face_send.at[turn, k, slot],
            recv_sem=face_recv.at[turn, k, slot],
            device_id=(me_b, part(offset)),
            device_id_type=MESH,
        )

    def operate_faces(turn, k, vectors, half):
        for at in range(half * 2 * shared, (half + 1) * 2 * shared, tile):
            part_sum = dot(dense[at:at + tile, :], vectors[k])
            summed[k, at:at + tile, :] = part_sum
            rounded = part_sum.astype(BF16)
            for block in range(4):
                low = max(at, block * shared)
                high = min(at + tile, (block + 1) * shared)
                if low < high:
                    leaving[turn, k, block, low - block * shared:high - block * shared, :] = rounded[low - at:high - at]
        for route in routes:
            if route[0] // 2 == half:
                face_copy(turn, k, route).start()

    def receive(k):
        for offset in range(1, bands):
            row_copy(k, offset).wait()

    def pick(low, high, cell):
        span = pl.ds(pl.multiple_of(cell * size, 128), size)
        node = across(columns[low:high, :], size)
        picked[:high - low, span] = dot(hot(node == cell_nodes[pl.ds(cell, 1), :]), ham[cell]).astype(BF16)

    def fill(low, high, span):
        dense[low:high, span] = dot(picked[:high - low, :], cell_hot[:, span]).astype(BF16)

    for face in range(4):
        columns[face * shared:(face + 1) * shared, :] = upright(face_nodes[face:face + 1, :])
    for cell in range(cells):
        at = nloc + cell * size
        columns[at:at + size, :] = upright(cell_nodes[cell:cell + 1, :])

    psi_load.wait()
    pl.semaphore_wait(barrier, bands + 3)
    turn(0)
    for k in range(1, count):
        for offset in range(1, bands):
            ritz_load(offset, k).start()
    for k in range(count):
        ritz_load(0, k).start()
    ham_load.wait()
    half = 2 * shared

    @pl.loop(0, cells, unroll=2)
    def _(cell):
        pick(half, face_rows, cell)

    if count > 1:
        turn(1)

    @pl.loop(0, nloc // step, unroll=2)
    def _(block):
        at = pl.multiple_of(block * step, step)
        numbers = lax.broadcasted_iota(jnp.int32, (total, step), 1) + at
        cell_hot[:, pl.ds(at, step)] = hot(numbers == across(columns[nloc:, :], step))
        fill(half, face_rows, pl.ds(at, step))

    keep(0)

    @pl.loop(0, cells, unroll=2)
    def _(cell):
        pick(0, half, cell)

    receive(0)
    operate_faces(0, 0, arrived, 1)

    @pl.loop(0, nloc // step, unroll=2)
    def _(block):
        at = pl.multiple_of(block * step, step)
        fill(0, half, pl.ds(at, step))
        match = lax.broadcasted_iota(jnp.int32, (face_rows, step), 1) + at == across(columns[:face_rows, :], step)
        order_hot[:face_rows, pl.ds(at, step)] = hot(match)
        places = lax.broadcasted_iota(jnp.int32, (face_rows, step), 0) + 1
        found[:, pl.ds(at, step)] = jnp.sum(jnp.where(match, places, 0), axis=0, keepdims=True)

    operate_faces(0, 0, arrived, 0)

    @pl.loop(2, count)
    def _(k):
        turn(k)

    if count > 1:
        keep(1)

    inner = jnp.where(found[...] == 0, 1, 0)
    before = jnp.broadcast_to(inner, (8, nloc))
    eight = lax.broadcasted_iota(jnp.int32, (8, nloc), 1)
    shift = 1
    while shift < nloc:
        before = before + jnp.where(eight >= shift, pltpu.roll(before, shift, 1), 0)
        shift *= 2
    place = jnp.where(found[...] == 0, before[:1, :] + (face_rows - 1), found[...] - 1)

    @pl.loop(face_rows // step, nloc // step)
    def _(block):
        at = pl.multiple_of(block * step, step)
        nodes = lax.broadcasted_iota(jnp.int32, (step, nloc), 1)
        match = lax.broadcasted_iota(jnp.int32, (step, nloc), 0) + at == place
        order_hot[pl.ds(at, step), :] = hot(match)
        node = jnp.sum(jnp.where(match, nodes, 0), axis=1, keepdims=True)
        columns[pl.ds(at, step), :] = jnp.broadcast_to(node, (step, 128))

    if count > 1:
        receive(1)
        operate_faces(0, 1, arrived, 1)
        operate_faces(0, 1, arrived, 0)

    low = face_rows
    while low < nloc:
        high = min(low + half, nloc)

        @pl.loop(0, cells, unroll=2)
        def _(cell, low=low, high=high):
            pick(low, high, cell)

        if high == nloc:
            columns[:nloc, :] = upright(place)

        @pl.loop(0, nloc // step, unroll=2)
        def _(block, low=low, high=high):
            at = pl.multiple_of(block * step, step)
            if high == nloc:
                numbers = lax.broadcasted_iota(jnp.int32, (nloc, step), 1) + at
                place_hot[:, pl.ds(at, step)] = hot(numbers == across(columns[:nloc, :], step))
            fill(low, high, pl.ds(at, step))

        low = high

    def order(k):
        for at in range(0, nloc, tile):
            rotated[k, at:at + tile, :] = dot(order_hot[at:at + tile, :], arrived[k]).astype(BF16)

    def inner_first(k):
        for at in range(face_rows, nloc, tile):
            part_sum = dot(dense[at:at + tile, :], arrived[k])
            first[k, at:at + tile, :] = ((part_sum - 0.25 * rotated[k, at:at + tile, :].astype(F32)) / 2.0).astype(BF16)

    def assembled(turn, k, slot):
        at = slice(slot * shared, (slot + 1) * shared)
        return summed[k, at, :] + landing[turn, k, slot].astype(F32)

    def result(value, k, at):
        return (2.0 * (value - 0.25 * first[k, at, :].astype(F32)) / 2.0 - rotated[k, at, :].astype(F32)).astype(BF16)

    def advance(k):
        for route in routes[::-1]:
            face_copy(0, k, route).wait()
            at = slice(route[1] * shared, (route[1] + 1) * shared)
            first[k, at, :] = ((assembled(0, k, route[1]) - 0.25 * rotated[k, at, :].astype(F32)) / 2.0).astype(BF16)
        for at in range(0, nloc, tile):
            arrived[k, at:at + tile, :] = dot(place_hot[at:at + tile, :], first[k]).astype(BF16)
        operate_faces(1, k, arrived, 1)
        operate_faces(1, k, arrived, 0)

    def put(k):
        return pltpu.make_async_copy(arrived.at[k], out.at[:, chunk(k)], store.at[k])

    def inner_result(k):
        for at in range(face_rows, nloc, tile):
            part_sum = dot(dense[at:at + tile, :], arrived[k])
            rotated[k, at:at + tile, :] = result(part_sum, k, slice(at, at + tile))

    def finish(k):
        for route in routes[::-1]:
            face_copy(1, k, route).wait()
            at = slice(route[1] * shared, (route[1] + 1) * shared)
            rotated[k, at, :] = result(assembled(1, k, route[1]), k, at)
        for at in range(0, nloc, tile):
            arrived[k, at:at + tile, :] = dot(place_hot[at:at + tile, :], rotated[k]).astype(BF16)
        put(k).start()

    @pl.loop(0, count)
    def _(k):
        @pl.when(k + 2 < count)
        def _():
            keep(k + 2)
            receive(k + 2)
            operate_faces(0, k + 2, arrived, 1)
            operate_faces(0, k + 2, arrived, 0)

        order(k)
        inner_first(k)
        advance(k)
        inner_result(k)

    @pl.loop(0, count)
    def _(k):
        finish(k)

    @pl.loop(0, count)
    def _(k):
        put(k).wait()


def copy_kernel(source, target, held, taken, given):
    pieces, rows = held.shape[0], held.shape[1]

    def take(i):
        return pltpu.make_async_copy(source.at[i * rows:(i + 1) * rows, :], held.at[i], taken.at[i])

    def give(i):
        return pltpu.make_async_copy(held.at[i], target.at[i * rows:(i + 1) * rows, :], given.at[i])

    for i in range(pieces):
        take(i).start()
    for i in range(pieces):
        take(i).wait()
        give(i).start()
    for i in range(pieces):
        give(i).wait()


def local(bands, parts, psi, ritz, cell_ham, cell_nodes, face_nodes):
    rows = psi.shape[1]
    nloc = rows * bands
    group = ritz.shape[1] // bands
    cells, size = cell_ham.shape[1], cell_ham.shape[2]
    shared = face_nodes.shape[2]
    width = 256 if group % 256 == 0 else 128
    count = group // width
    anywhere = pl.BlockSpec(memory_space=pl.ANY)
    vmem = pl.BlockSpec(memory_space=pltpu.VMEM)

    out = pl.pallas_call(
        functools.partial(kernel, bands, parts),
        out_shape=jax.ShapeDtypeStruct((nloc, group), BF16),
        in_specs=[anywhere] * 3 + [vmem] * 2,
        out_specs=anywhere,
        scratch_shapes=[
            pltpu.VMEM((rows, ritz.shape[0]), BF16),
            pltpu.VMEM((bands, count, ritz.shape[0], width), BF16),
            pltpu.VMEM((cells, size, size), BF16),
            pltpu.VMEM((bands - 1, count, rows, width), BF16),
            pltpu.VMEM((count, nloc, width), BF16),
            pltpu.VMEM((count, nloc, width), BF16),
            pltpu.VMEM((count, nloc, width), BF16),
            pltpu.VMEM((count, 4 * shared, width), F32),
            pltpu.VMEM((2, count, 4, shared, width), BF16),
            pltpu.VMEM((2, count, 4, shared, width), BF16),
            pltpu.VMEM((cells * size, nloc), BF16),
            pltpu.VMEM((2 * shared, cells * size), BF16),
            pltpu.VMEM((nloc, nloc), BF16),
            pltpu.VMEM((nloc, nloc), BF16),
            pltpu.VMEM((nloc, nloc), BF16),
            pltpu.VMEM((nloc + cells * size, 128), jnp.int32),
            pltpu.VMEM((1, nloc), jnp.int32),
            pltpu.SemaphoreType.DMA((2 + bands * count,)),
            pltpu.SemaphoreType.DMA((count,)),
            pltpu.SemaphoreType.DMA((bands - 1, count)),
            pltpu.SemaphoreType.DMA((bands - 1, count)),
            pltpu.SemaphoreType.DMA((2, count, 4)),
            pltpu.SemaphoreType.DMA((2, count, 4)),
        ],
        compiler_params=pltpu.CompilerParams(
            collective_id=0, has_side_effects=True, vmem_limit_bytes=62 * 1024 * 1024
        ),
    )(psi[0], ritz, cell_ham[0], cell_nodes[0], face_nodes[0])
    pieces = 6 if nloc % 48 == 0 else 1
    out = pl.pallas_call(
        copy_kernel,
        out_shape=jax.ShapeDtypeStruct((nloc, group), BF16),
        in_specs=[anywhere],
        out_specs=anywhere,
        scratch_shapes=[
            pltpu.VMEM((pieces, nloc // pieces, group), BF16),
            pltpu.SemaphoreType.DMA((pieces,)),
            pltpu.SemaphoreType.DMA((pieces,)),
        ],
    )(out)
    return out[None]


def solution(mesh):
    return jax.shard_map(
        functools.partial(local, mesh.shape["band"], mesh.shape["mesh"]),
        mesh=mesh,
        in_specs=(
            P("mesh", "band", None),
            P(),
            P("mesh", None, None, None),
            P("mesh", None, None),
            P("mesh", None, None),
        ),
        out_specs=P("mesh", None, "band"),
        check_vma=False,
    )
```

```python
import functools
import math

import jax
import jax.numpy as jnp
from jax import lax
from jax.experimental import pallas as pl
from jax.experimental.pallas import tpu as pltpu
from jax.sharding import PartitionSpec as P

GRID_W = 4
MESH = pl.DeviceIdType.MESH
BF16 = jnp.bfloat16
F32 = jnp.float32


def dot(a, b):
    return jnp.dot(a, b, preferred_element_type=F32)


def hot(condition):
    return jnp.where(condition, 1.0, 0.0).astype(BF16)


def upright(row):
    return jnp.broadcast_to(row, (128, row.shape[1])).T


def across(column, width):
    return jnp.concatenate([column] * (width // 128), axis=1)


def kernel(bands, parts, psi_hbm, ritz_hbm, ham_hbm, cell_nodes, face_nodes, out,
           psi, ritz, ham, turned, arrived, rotated, first, summed, leaving, landing,
           cell_hot, picked, dense, order_hot, place_hot, columns, found,
           load, store, row_send, row_recv, face_send, face_recv):
    me_b = lax.axis_index("band")
    me_p = lax.axis_index("mesh")
    rows = psi.shape[0]
    count, nloc, width = arrived.shape
    group = count * width
    shared = face_nodes.shape[1]
    face_rows = 4 * shared
    cells, size = ham.shape[0], ham.shape[1]
    total = cells * size
    tile = math.gcd(2 * shared, nloc)
    step = 256

    routes = ((3, 2, GRID_W), (2, 3, -GRID_W), (1, 0, 1), (0, 1, -1))

    def part(offset):
        return lax.rem(me_p + offset + parts, parts)

    def partner(offset):
        return lax.rem(me_b + offset, bands)

    def ritz_load(offset, k):
        start = pl.multiple_of(partner(offset) * group + k * width, 128)
        return pltpu.make_async_copy(
            ritz_hbm.at[:, pl.ds(start, width)], ritz.at[offset, k], load.at[2 + offset * count + k])

    psi_load = pltpu.make_async_copy(psi_hbm, psi, load.at[0])
    ham_load = pltpu.make_async_copy(ham_hbm, ham, load.at[1])
    psi_load.start()
    for offset in range(1, bands):
        ritz_load(offset, 0).start()
    ham_load.start()

    barrier = pltpu.get_barrier_semaphore()
    for offset in range(1, bands):
        pl.semaphore_signal(barrier, inc=1, device_id=(partner(offset), me_p), device_id_type=MESH)
    for _, _, offset in routes:
        pl.semaphore_signal(barrier, inc=1, device_id=(me_b, part(offset)), device_id_type=MESH)

    def own_rows(k, owner):
        return arrived.at[k, pl.ds(pl.multiple_of(owner * rows, rows), rows), :]

    def row_copy(k, offset):
        return pltpu.make_async_remote_copy(
            src_ref=turned.at[offset - 1, k],
            dst_ref=own_rows(k, me_b),
            send_sem=row_send.at[offset - 1, k],
            recv_sem=row_recv.at[offset - 1, k],
            device_id=(partner(offset), me_p),
            device_id_type=MESH,
        )

    def chunk(k):
        return pl.ds(pl.multiple_of(k * width, 128), width)

    def turn(k):
        for offset in range(1, bands):
            ritz_load(offset, k).wait()
            turned[offset - 1, k] = dot(psi[...], ritz[offset, k]).astype(BF16)
            row_copy(k, offset).start()

    def keep(k):
        ritz_load(0, k).wait()
        own_rows(k, me_b)[...] = dot(psi[...], ritz[0, k]).astype(BF16)

    def face_copy(turn, k, route):
        block, slot, offset = route
        return pltpu.make_async_remote_copy(
            src_ref=leaving.at[turn, k, block],
            dst_ref=landing.at[turn, k, slot],
            send_sem=face_send.at[turn, k, slot],
            recv_sem=face_recv.at[turn, k, slot],
            device_id=(me_b, part(offset)),
            device_id_type=MESH,
        )

    def operate_faces(turn, k, vectors, half):
        for at in range(half * 2 * shared, (half + 1) * 2 * shared, tile):
            part_sum = dot(dense[at:at + tile, :], vectors[k])
            summed[k, at:at + tile, :] = part_sum
            rounded = part_sum.astype(BF16)
            for block in range(4):
                low = max(at, block * shared)
                high = min(at + tile, (block + 1) * shared)
                if low < high:
                    leaving[turn, k, block, low - block * shared:high - block * shared, :] = rounded[low - at:high - at]
        for route in routes:
            if route[0] // 2 == half:
                face_copy(turn, k, route).start()

    def receive(k):
        for offset in range(1, bands):
            row_copy(k, offset).wait()

    def pick(low, high, cell):
        span = pl.ds(pl.multiple_of(cell * size, 128), size)
        node = across(columns[low:high, :], size)
        picked[:high - low, span] = dot(hot(node == cell_nodes[pl.ds(cell, 1), :]), ham[cell]).astype(BF16)

    def fill(low, high, span):
        dense[low:high, span] = dot(picked[:high - low, :], cell_hot[:, span]).astype(BF16)

    for face in range(4):
        columns[face * shared:(face + 1) * shared, :] = upright(face_nodes[face:face + 1, :])
    for cell in range(cells):
        at = nloc + cell * size
        columns[at:at + size, :] = upright(cell_nodes[cell:cell + 1, :])

    psi_load.wait()
    pl.semaphore_wait(barrier, bands + 3)
    turn(0)
    for k in range(1, count):
        for offset in range(1, bands):
            ritz_load(offset, k).start()
    for k in range(count):
        ritz_load(0, k).start()
    ham_load.wait()
    half = 2 * shared

    @pl.loop(0, cells, unroll=2)
    def _(cell):
        pick(half, face_rows, cell)

    if count > 1:
        turn(1)

    @pl.loop(0, nloc // step, unroll=2)
    def _(block):
        at = pl.multiple_of(block * step, step)
        numbers = lax.broadcasted_iota(jnp.int32, (total, step), 1) + at
        cell_hot[:, pl.ds(at, step)] = hot(numbers == across(columns[nloc:, :], step))
        fill(half, face_rows, pl.ds(at, step))

    keep(0)

    @pl.loop(0, cells, unroll=2)
    def _(cell):
        pick(0, half, cell)

    receive(0)
    operate_faces(0, 0, arrived, 1)

    @pl.loop(0, nloc // step, unroll=2)
    def _(block):
        at = pl.multiple_of(block * step, step)
        fill(0, half, pl.ds(at, step))
        match = lax.broadcasted_iota(jnp.int32, (face_rows, step), 1) + at == across(columns[:face_rows, :], step)
        order_hot[:face_rows, pl.ds(at, step)] = hot(match)
        places = lax.broadcasted_iota(jnp.int32, (face_rows, step), 0) + 1
        found[:, pl.ds(at, step)] = jnp.sum(jnp.where(match, places, 0), axis=0, keepdims=True)

    operate_faces(0, 0, arrived, 0)

    @pl.loop(2, count)
    def _(k):
        turn(k)

    if count > 1:
        keep(1)

    inner = jnp.where(found[...] == 0, 1, 0)
    before = jnp.broadcast_to(inner, (8, nloc))
    eight = lax.broadcasted_iota(jnp.int32, (8, nloc), 1)
    shift = 1
    while shift < nloc:
        before = before + jnp.where(eight >= shift, pltpu.roll(before, shift, 1), 0)
        shift *= 2
    place = jnp.where(found[...] == 0, before[:1, :] + (face_rows - 1), found[...] - 1)

    @pl.loop(face_rows // step, nloc // step)
    def _(block):
        at = pl.multiple_of(block * step, step)
        nodes = lax.broadcasted_iota(jnp.int32, (step, nloc), 1)
        match = lax.broadcasted_iota(jnp.int32, (step, nloc), 0) + at == place
        order_hot[pl.ds(at, step), :] = hot(match)
        node = jnp.sum(jnp.where(match, nodes, 0), axis=1, keepdims=True)
        columns[pl.ds(at, step), :] = jnp.broadcast_to(node, (step, 128))

    low = face_rows
    while low < nloc:
        high = min(low + half, nloc)

        @pl.loop(0, cells, unroll=2)
        def _(cell, low=low, high=high):
            pick(low, high, cell)

        if high == nloc:
            columns[:nloc, :] = upright(place)
        if low == face_rows and count > 1:
            receive(1)
            operate_faces(0, 1, arrived, 1)
            operate_faces(0, 1, arrived, 0)

        @pl.loop(0, nloc // step, unroll=2)
        def _(block, low=low, high=high):
            at = pl.multiple_of(block * step, step)
            if high == nloc:
                numbers = lax.broadcasted_iota(jnp.int32, (nloc, step), 1) + at
                place_hot[:, pl.ds(at, step)] = hot(numbers == across(columns[:nloc, :], step))
            fill(low, high, pl.ds(at, step))

        low = high

    def order(k):
        for at in range(0, nloc, tile):
            rotated[k, at:at + tile, :] = dot(order_hot[at:at + tile, :], arrived[k]).astype(BF16)

    def inner_first(k):
        for at in range(face_rows, nloc, tile):
            part_sum = dot(dense[at:at + tile, :], arrived[k])
            first[k, at:at + tile, :] = ((part_sum - 0.25 * rotated[k, at:at + tile, :].astype(F32)) / 2.0).astype(BF16)

    def assembled(turn, k, slot):
        at = slice(slot * shared, (slot + 1) * shared)
        return summed[k, at, :] + landing[turn, k, slot].astype(F32)

    def result(value, k, at):
        return (2.0 * (value - 0.25 * first[k, at, :].astype(F32)) / 2.0 - rotated[k, at, :].astype(F32)).astype(BF16)

    def advance(k):
        for route in routes[::-1]:
            face_copy(0, k, route).wait()
            at = slice(route[1] * shared, (route[1] + 1) * shared)
            first[k, at, :] = ((assembled(0, k, route[1]) - 0.25 * rotated[k, at, :].astype(F32)) / 2.0).astype(BF16)
        for at in range(0, nloc, tile):
            arrived[k, at:at + tile, :] = dot(place_hot[at:at + tile, :], first[k]).astype(BF16)
        operate_faces(1, k, arrived, 0)
        operate_faces(1, k, arrived, 1)

    def put(k):
        return pltpu.make_async_copy(arrived.at[k], out.at[:, chunk(k)], store.at[k])

    def inner_result(k):
        for at in range(face_rows, nloc, tile):
            part_sum = dot(dense[at:at + tile, :], arrived[k])
            rotated[k, at:at + tile, :] = result(part_sum, k, slice(at, at + tile))

    def finish(k):
        for route in routes[::-1]:
            face_copy(1, k, route).wait()
            at = slice(route[1] * shared, (route[1] + 1) * shared)
            rotated[k, at, :] = result(assembled(1, k, route[1]), k, at)
        for at in range(0, nloc, tile):
            arrived[k, at:at + tile, :] = dot(place_hot[at:at + tile, :], rotated[k]).astype(BF16)
        put(k).start()

    @pl.loop(0, count)
    def _(k):
        @pl.when(k + 2 < count)
        def _():
            keep(k + 2)
            receive(k + 2)
            operate_faces(0, k + 2, arrived, 1)
            operate_faces(0, k + 2, arrived, 0)

        order(k)
        inner_first(k)
        advance(k)
        inner_result(k)

    @pl.loop(0, count)
    def _(k):
        finish(k)

    @pl.loop(0, count)
    def _(k):
        put(k).wait()


def copy_kernel(source, target, held, taken, given):
    pieces, rows = held.shape[0], held.shape[1]

    def take(i):
        return pltpu.make_async_copy(source.at[i * rows:(i + 1) * rows, :], held.at[i], taken.at[i])

    def give(i):
        return pltpu.make_async_copy(held.at[i], target.at[i * rows:(i + 1) * rows, :], given.at[i])

    for i in range(pieces):
        take(i).start()
    for i in range(pieces):
        take(i).wait()
        give(i).start()
    for i in range(pieces):
        give(i).wait()


def local(bands, parts, psi, ritz, cell_ham, cell_nodes, face_nodes):
    rows = psi.shape[1]
    nloc = rows * bands
    group = ritz.shape[1] // bands
    cells, size = cell_ham.shape[1], cell_ham.shape[2]
    shared = face_nodes.shape[2]
    width = 256 if group % 256 == 0 else 128
    count = group // width
    anywhere = pl.BlockSpec(memory_space=pl.ANY)
    vmem = pl.BlockSpec(memory_space=pltpu.VMEM)

    out = pl.pallas_call(
        functools.partial(kernel, bands, parts),
        out_shape=jax.ShapeDtypeStruct((nloc, group), BF16),
        in_specs=[anywhere] * 3 + [vmem] * 2,
        out_specs=anywhere,
        scratch_shapes=[
            pltpu.VMEM((rows, ritz.shape[0]), BF16),
            pltpu.VMEM((bands, count, ritz.shape[0], width), BF16),
            pltpu.VMEM((cells, size, size), BF16),
            pltpu.VMEM((bands - 1, count, rows, width), BF16),
            pltpu.VMEM((count, nloc, width), BF16),
            pltpu.VMEM((count, nloc, width), BF16),
            pltpu.VMEM((count, nloc, width), BF16),
            pltpu.VMEM((count, 4 * shared, width), F32),
            pltpu.VMEM((2, count, 4, shared, width), BF16),
            pltpu.VMEM((2, count, 4, shared, width), BF16),
            pltpu.VMEM((cells * size, nloc), BF16),
            pltpu.VMEM((2 * shared, cells * size), BF16),
            pltpu.VMEM((nloc, nloc), BF16),
            pltpu.VMEM((nloc, nloc), BF16),
            pltpu.VMEM((nloc, nloc), BF16),
            pltpu.VMEM((nloc + cells * size, 128), jnp.int32),
            pltpu.VMEM((1, nloc), jnp.int32),
            pltpu.SemaphoreType.DMA((2 + bands * count,)),
            pltpu.SemaphoreType.DMA((count,)),
            pltpu.SemaphoreType.DMA((bands - 1, count)),
            pltpu.SemaphoreType.DMA((bands - 1, count)),
            pltpu.SemaphoreType.DMA((2, count, 4)),
            pltpu.SemaphoreType.DMA((2, count, 4)),
        ],
        compiler_params=pltpu.CompilerParams(
            collective_id=0, has_side_effects=True, vmem_limit_bytes=62 * 1024 * 1024
        ),
    )(psi[0], ritz, cell_ham[0], cell_nodes[0], face_nodes[0])
    pieces = 6 if nloc % 48 == 0 else 1
    out = pl.pallas_call(
        copy_kernel,
        out_shape=jax.ShapeDtypeStruct((nloc, group), BF16),
        in_specs=[anywhere],
        out_specs=anywhere,
        scratch_shapes=[
            pltpu.VMEM((pieces, nloc // pieces, group), BF16),
            pltpu.SemaphoreType.DMA((pieces,)),
            pltpu.SemaphoreType.DMA((pieces,)),
        ],
    )(out)
    return out[None]


def solution(mesh):
    return jax.shard_map(
        functools.partial(local, mesh.shape["band"], mesh.shape["mesh"]),
        mesh=mesh,
        in_specs=(
            P("mesh", "band", None),
            P(),
            P("mesh", None, None, None),
            P("mesh", None, None),
            P("mesh", None, None),
        ),
        out_specs=P("mesh", None, "band"),
        check_vma=False,
    )
```
